128 devices in a mesh: dp: 16 (over y_hi, x, core), tensor: 8 (over z, y_lo).
Axes of the slice: x: 4, y: 4 (y_hi: 2, y_lo: 2; y = y_hi * 2 + y_lo), z: 4, core: 2. Of those that a mesh axis runs over, the one named last changes fastest.
Arguments:
- inputs: bfloat16 [2048, 8192], P('dp', 'tensor'), may hold values from -6 to 6
- out_grad: bfloat16 [2048, 8192], P('dp', 'tensor'), may hold values from -6 to 6
- weights: bfloat16 [3, 768, 128, 128], P(None, 'tensor'), may hold values from -0.1875 to 0.1875
- block_index: int32 [3, 768, 2], P(None, 'tensor'), may hold values from 0 to 63, as said below
- block_counts: int32 [8, 3], P('tensor'), may hold values from 38 to 96, as said below
- first_moment: float32 [3, 768, 128, 128], P(None, ('tensor', 'dp')), may hold values from -120 to 120
- second_moment: float32 [3, 768, 128, 128], P(None, ('tensor', 'dp')), may hold values from 100 to 10000
Outputs:
- outputs: bfloat16 [2048, 8192], P('dp', 'tensor')
- input_grad: bfloat16 [2048, 8192], P('dp', 'tensor')
- update: float32 [3, 768, 128, 128], P(None, ('tensor', 'dp'))
The draws below stay inside these ranges and needn't reach their ends.
Inputs may be any that keep to these rules, and one draw needn't show every extreme that they name: block_index[k, t * 96 + j, 0] is a feature block (below 64) and block_index[k, t * 96 + j, 1] a hidden block of tensor index t (below 14); the 96 slots of one matrix on one tensor index name distinct blocks. block_counts[t, k] live slots of matrix k on tensor index t; for each matrix some tensor index has exactly 96.
All inputs are finite; a program needn't handle non-finite values.
Results may differ from the reference program's by a relative error of at most 0.013.
Values may be sent and summed in bfloat16 or wider, within the bound.
A program may use at most 128 MiB of HBM per device.

```python
import math
import jax
import jax.numpy as jnp
from jax import lax

D = 8192
BLK = 128
DBLK = 64
HB_DEV = 14
CAP = 96
TOK_DEV = 128
TOKENS = 2048
N_DP = 16
N_TENSOR = 8


def shuffled_blocks(device_key):
    position_count = DBLK * HB_DEV
    shuffled = jax.random.permutation(device_key, position_count)[:CAP]
    positions = (shuffled + (position_count - 1 - shuffled[0])) % position_count
    return jnp.stack([positions // HB_DEV, positions % HB_DEV], axis=-1).astype(jnp.int32)


def draw_block_index(key, part):
    device_keys = jax.random.split(jax.random.fold_in(key, 11), 3 * N_TENSOR)
    return jax.vmap(shuffled_blocks)(device_keys).reshape(3, N_TENSOR * CAP, 2)


def draw_block_counts(key, part):
    count_key = jax.random.fold_in(key, 23)
    counts_drawn = jax.random.randint(jax.random.fold_in(count_key, 1), (N_TENSOR, 3), CAP * 2 // 5, CAP + 1)
    fullest = jax.random.randint(jax.random.fold_in(count_key, 2), (3,), 0, N_TENSOR)
    fullest_rows = jnp.arange(N_TENSOR)[:, None] == fullest[None, :]
    return jnp.where(fullest_rows, CAP, counts_drawn).astype(jnp.int32)


def block_scale(rng, extent, pieces, least, largest):
    loudness, own = 1.0, jax.random.fold_in(rng, 6)
    for dim, shards_of in pieces:
        heights = jnp.exp(jax.random.uniform(jax.random.fold_in(own, dim), (shards_of,), jnp.float32, least / len(pieces), largest / len(pieces)))
        loudness = loudness * jnp.repeat(heights, extent[dim] // shards_of).reshape([-1 if axis == dim else 1 for axis in range(len(extent))])
    return loudness


def gaussian(stream_key, extent, scale, reach, shards=(), held_as=jnp.bfloat16):
    factor_of = block_scale(stream_key, extent, shards, -0.22, 0.18) if shards else 1.0
    result = jax.random.normal(stream_key, extent, jnp.float32) * scale * factor_of
    return jnp.minimum(jnp.maximum(result, -reach), reach).astype(held_as)


def setup_inputs(seed: int = 0) -> dict:
    splits = jax.random.split(jax.random.key(seed), 8)
    inputs = gaussian(splits[0], (TOKENS, D), 1.0, 6.0, ((0, 16), (1, 8)))
    out_grad = gaussian(splits[1], (TOKENS, D), 1.0, 6.0, ((0, 16), (1, 8)))
    weights = gaussian(splits[2], (3, N_TENSOR * CAP, BLK, BLK), (D // 8) ** -0.5, 0.1875, ((1, 8),))
    block_index = draw_block_index(jax.random.fold_in(splits[7], 71), 0)
    block_counts = draw_block_counts(jax.random.fold_in(splits[7], 71), 0)
    first_moment = gaussian(splits[5], (3, N_TENSOR * CAP, BLK, BLK), 20.0, 120.0, ((1, 128),), jnp.float32)
    second_moment = jnp.clip(jnp.exp(math.log(10000.0) - 4.6051702 * jax.random.uniform(splits[6], (3, N_TENSOR * CAP, BLK, BLK), jnp.float32) ** block_scale(splits[6], (3, N_TENSOR * CAP, BLK, BLK), ((1, 128),), -0.2, 0.2)), 100.0, 10000.0)
    return dict(inputs=inputs, out_grad=out_grad, weights=weights, block_index=block_index, block_counts=block_counts, first_moment=first_moment, second_moment=second_moment)


EPSILON = 1e-08

def reference(inputs, out_grad, weights, block_index, block_counts, first_moment, second_moment):
    input_blocks = inputs.reshape(TOKENS, DBLK, BLK)
    cotangent_blocks = out_grad.reshape(TOKENS, DBLK, BLK)
    device_weights = weights.reshape(3, N_TENSOR, CAP, BLK, BLK).transpose(1, 0, 2, 3, 4)
    device_index = block_index.reshape(3, N_TENSOR, CAP, 2).transpose(1, 0, 2, 3)
    first_prev = first_moment.reshape(3, N_TENSOR, CAP, BLK, BLK).transpose(1, 0, 2, 3, 4)
    second_prev = second_moment.reshape(3, N_TENSOR, CAP, BLK, BLK).transpose(1, 0, 2, 3, 4)
    slot_ids = jnp.arange(CAP, dtype=jnp.int32)
    hidden_ids = jnp.arange(HB_DEV, dtype=jnp.int32)
    feature_ids = jnp.arange(DBLK, dtype=jnp.int32)

    def replica_sum(left_rows, right_rows):
        left_rows = left_rows.reshape(N_DP, TOK_DEV, CAP, BLK)
        right_rows = right_rows.reshape(N_DP, TOK_DEV, CAP, BLK)
        replica_terms = jnp.einsum('rtsk,rtsn->rskn', left_rows, right_rows)
        replica_terms = lax.optimization_barrier(replica_terms.astype(jnp.bfloat16)).astype(jnp.float32)
        return lax.optimization_barrier(jnp.sum(replica_terms, axis=0))

    def per_device(running, device_items):
        out_sum, in_sum = running
        block_values, index_here, counts_here, first_here, second_here = device_items
        live_slots = (slot_ids[None, :] < counts_here[:, None]).astype(jnp.float32)
        hidden_select = (index_here[:, :, 1, None] == hidden_ids).astype(jnp.float32) * live_slots[:, :, None]
        feature_select = (index_here[:, :, 0, None] == feature_ids).astype(jnp.float32) * live_slots[:, :, None]
        values_wide = block_values.astype(jnp.float32)
        gate_inputs = input_blocks[:, index_here[0, :, 0], :].astype(jnp.float32)
        up_inputs = input_blocks[:, index_here[1, :, 0], :].astype(jnp.float32)
        gate_proj = jnp.einsum('tsn,sh->thn', jnp.einsum('tsk,skn->tsn', gate_inputs, values_wide[0]), hidden_select[0])
        up_proj = jnp.einsum('tsn,sh->thn', jnp.einsum('tsk,skn->tsn', up_inputs, values_wide[1]), hidden_select[1])
        sigmoid_gate = jax.nn.sigmoid(gate_proj)
        activated = gate_proj * sigmoid_gate
        hidden = (activated * up_proj).astype(jnp.bfloat16)
        down_inputs = hidden[:, index_here[2, :, 1], :].astype(jnp.float32)
        out_partial = jnp.einsum('tsn,sf->tfn', jnp.einsum('tsk,skn->tsn', down_inputs, values_wide[2]), feature_select[2])
        out_partial = out_partial.reshape(TOKENS, D)
        out_sum = out_sum + lax.optimization_barrier(out_partial.astype(jnp.bfloat16)).astype(jnp.float32)
        down_cotangents = cotangent_blocks[:, index_here[2, :, 0], :].astype(jnp.float32)
        hidden_grad = jnp.einsum('tsk,sh->thk', jnp.einsum('tsn,skn->tsk', down_cotangents, values_wide[2]), hidden_select[2])
        gate_grad_rows = (hidden_grad * up_proj * sigmoid_gate * (1.0 + gate_proj * (1.0 - sigmoid_gate))).astype(jnp.bfloat16)
        up_grad_rows = (hidden_grad * activated).astype(jnp.bfloat16)
        gate_back = gate_grad_rows[:, index_here[0, :, 1], :].astype(jnp.float32)
        up_back = up_grad_rows[:, index_here[1, :, 1], :].astype(jnp.float32)
        in_partial = jnp.einsum('tsk,sf->tfk', jnp.einsum('tsn,skn->tsk', gate_back, values_wide[0]), feature_select[0])
        in_partial = in_partial + jnp.einsum('tsk,sf->tfk', jnp.einsum('tsn,skn->tsk', up_back, values_wide[1]), feature_select[1])
        in_partial = in_partial.reshape(TOKENS, D)
        in_sum = in_sum + lax.optimization_barrier(in_partial.astype(jnp.bfloat16)).astype(jnp.float32)
        gradients = jnp.stack([replica_sum(gate_inputs, gate_back), replica_sum(up_inputs, up_back), replica_sum(down_inputs, down_cotangents)])
        gradients = gradients * live_slots[:, :, None, None]
        first_new = 0.9 * first_here + 0.1 * gradients
        second_new = 0.95 * second_here + 0.05 * gradients * gradients
        update = live_slots[:, :, None, None] * first_new / (jnp.sqrt(second_new) + EPSILON)
        return ((out_sum, in_sum), update)
    zero_sums = jnp.zeros((TOKENS, D), jnp.float32)
    results, updates = lax.scan(per_device, (zero_sums, zero_sums), (device_weights, device_index, block_counts, first_prev, second_prev))
    update = updates.transpose(1, 0, 2, 3, 4).reshape(3, N_TENSOR * CAP, BLK, BLK)
    return (results[0].astype(jnp.bfloat16), results[1].astype(jnp.bfloat16), update)
```

```python
import functools

import jax
import jax.numpy as jnp
from jax import lax
from jax.experimental import pallas as pl
from jax.experimental.pallas import tpu as pltpu
from jax.sharding import PartitionSpec as P

MESH = pl.DeviceIdType.MESH
EPSILON = 1e-08
HB = 14
CAP = 96
DB = 64
B = 128
ZERO = 192

L_X, L_OG, L_W, L_M, L_OUT = 0, 8, 16, 19, 21
N_LOCAL = 24
R_X, R_OG, R_O, R_I, R_G, R_CORE = 0, 8, 16, 23, 30, 51
N_REMOTE = 63


def slot_lists(block_index, counts):
    feature, hid = block_index[:, :, 0], block_index[:, :, 1]
    slot = jnp.arange(CAP, dtype=jnp.int32)
    live = slot[None, :] < counts[0][:, None]

    def padded(target, source, weight, alive):
        pad = 2 * CAP - target.shape[0]
        packed = weight | (source << 9) | (jnp.where(alive, target, DB) << 16)
        return jnp.pad(packed, (0, pad), constant_values=DB << 16)

    both = lambda a, b: jnp.concatenate([a, b])
    packed = jnp.stack(
        [
            padded(hid[0], feature[0], slot, live[0]),
            padded(hid[1], feature[1], slot + CAP, live[1]),
            padded(hid[2], feature[2], slot + 2 * CAP, live[2]),
            padded(feature[2], hid[2], slot + 2 * CAP, live[2]),
            padded(
                both(feature[0], feature[1]),
                both(hid[0], hid[1] + HB),
                both(slot, slot + CAP),
                both(live[0], live[1]),
            ),
        ]
    )
    place = jnp.arange(2 * CAP, dtype=jnp.int32)
    key = (packed >> 16) * 256 + place[None, :]
    rank = jnp.sum((key[:, None, :] < key[:, :, None]).astype(jnp.int32), axis=2)
    ordered = jnp.sum(
        jnp.where(rank[:, None, :] == place[None, :, None], packed[:, None, :], 0), axis=2
    )
    target = ordered >> 16
    same = jnp.pad((target[:, 1:] == target[:, :-1]).astype(jnp.int32), ((0, 0), (1, 0)))
    lists = (ordered & 0xFFFF) | (same << 16)
    group = jnp.arange(DB, dtype=jnp.int32)
    upto = jnp.sum((key[:, None, :] < (group[None, :, None] + 1) * 256).astype(jnp.int32), axis=2)
    before = jnp.sum((key[:, None, :] < group[None, :, None] * 256).astype(jnp.int32), axis=2)
    base = jnp.array([0, CAP, CAP, 0, 0], jnp.int32)
    lasts = jnp.where(upto > before, upto - 1 + base[:, None], ZERO)
    pairs = feature | (hid << 8)
    return lists, lasts, pairs


def kernel(
    inputs, out_grad, weights, lists, lasts, pairs, counts, first, second,
    out_o, out_i, out_u,
    xb, gb, wb, sums, gate, up, hidden, rows, ob, ib, grads, core_in,
    ra_o, rb_o, rm_o, ra_g, rb_g, rm_g, mom,
    lsem, ssem, rsem,
):
    d, t = lax.axis_index("dp"), lax.axis_index("tensor")
    core, px, yh = d % 2, (d // 2) % 4, d // 8
    z, yl = t // 2, t % 2
    dev_core = (d + 1 - 2 * core, t)
    dev_xp = (yh * 8 + ((px + 1) % 4) * 2 + core, t)
    dev_xm = (yh * 8 + ((px + 3) % 4) * 2 + core, t)
    dev_yh = ((1 - yh) * 8 + px * 2 + core, t)
    dev_zp = (d, ((z + 1) % 4) * 2 + yl)
    dev_zm = (d, ((z + 3) % 4) * 2 + yl)
    dev_yl = (d, t + 1 - 2 * yl)

    def local(src, dst, sem):
        return pltpu.make_async_copy(src, dst, lsem.at[sem])

    def remote(src, dst, sem, dev):
        return pltpu.make_async_remote_copy(
            src_ref=src, dst_ref=dst, send_sem=ssem.at[sem], recv_sem=rsem.at[sem],
            device_id=dev, device_id_type=MESH,
        )

    sent = []

    def send(copy):
        copy.start()
        sent.append(copy)

    for i in range(8):
        local(inputs.at[:, pl.ds(i * B, B)], xb.at[t * 8 + i], L_X + i).start()
    for i in range(8):
        local(out_grad.at[:, pl.ds(i * B, B)], gb.at[t * 8 + i], L_OG + i).start()
    barrier = pltpu.get_barrier_semaphore()
    for dev in (dev_core, dev_xp, dev_xm, dev_yh, dev_zp, dev_zm, dev_yl):
        pl.semaphore_signal(barrier, inc=1, device_id=dev, device_id_type=MESH)
    for k in range(3):
        local(weights.at[k], wb.at[pl.ds(k * CAP, CAP)], L_W + k).start()
    local(first, mom.at[0], L_M).start()
    local(second, mom.at[1], L_M + 1).start()
    sums[ZERO] = jnp.zeros((B, B), jnp.float32)
    pl.semaphore_wait(barrier, 7)

    class Gather:
        def __init__(self, buf, base):
            chunk = lambda zz, yy, lo=0, n=8: buf.at[pl.ds((((zz + 4) % 4) * 2 + yy) * 8 + lo, n)]
            mk = lambda ref, sem, dev: remote(ref, ref, base + sem, dev)
            other = 1 - yl
            self.a = mk(chunk(z, yl), 0, dev_yl)
            self.bp = mk(chunk(z, yl), 1, dev_zp)
            self.bm = mk(chunk(z, yl), 2, dev_zm)
            self.cp = mk(chunk(z, other), 3, dev_zp)
            self.cm = mk(chunk(z, other), 4, dev_zm)
            self.dp = mk(chunk(z - 1, yl, 0, 4), 5, dev_zp)
            self.dm = mk(chunk(z + 1, yl, 4, 4), 6, dev_zm)
            self.e = mk(chunk(z + 2, yl), 7, dev_yl)

    class Reduce:
        def __init__(self, part, pos, pair, dev_p, dev_m, dev_pair, ra, rb, rm, base):
            nxt, opp, prv = (pos + 1) % 4, (pos + 2) % 4, (pos + 3) % 4
            self.part, self.pos, self.pair = part, pos, pair
            self.nxt, self.prv = nxt, prv
            self.ra, self.rb, self.rm = ra, rb, rm
            self.ap = remote(part(0, opp), ra.at[0], base, dev_p)
            self.am = remote(part(1, opp), ra.at[1], base + 1, dev_m)
            self.bp0 = remote(part(0, nxt), rb.at[0, 0], base + 2, dev_p)
            self.bp1 = remote(part(1, nxt), rb.at[0, 1], base + 3, dev_p)
            self.bm0 = remote(part(0, prv), rb.at[1, 0], base + 4, dev_m)
            self.bm1 = remote(part(1, prv), rb.at[1, 1], base + 5, dev_m)
            self.m = remote(part(1 - pair, pos), rm, base + 6, dev_pair)
            self.n = rm.shape[0]

        def start(self):
            send(self.ap)
            send(self.am)
            send(self.bp1)
            send(self.bm0)

        def relay(self):
            self.ap.wait_recv()
            add_into(self.part(0, self.nxt), self.ra.at[0], self.n)
            send(self.bp0)
            self.am.wait_recv()
            add_into(self.part(1, self.prv), self.ra.at[1], self.n)
            send(self.bm1)

        def cross(self):
            for b in (self.bp0, self.bp1, self.bm0, self.bm1):
                b.wait_recv()
            far = 1 - self.pair
            mine = self.part(far, self.pos)

            def body(i, carry):
                v = mine[i].astype(jnp.float32) + self.rb[0, far, i].astype(jnp.float32)
                mine[i] = (v + self.rb[1, far, i].astype(jnp.float32)).astype(jnp.bfloat16)
                return carry

            lax.fori_loop(0, self.n, body, 0)
            send(self.m)

        def total(self, i):
            mine = self.part(self.pair, self.pos)
            v = mine[i].astype(jnp.float32) + self.rb[0, self.pair, i].astype(jnp.float32)
            v = v + self.rb[1, self.pair, i].astype(jnp.float32)
            return v + self.rm[i].astype(jnp.float32)

    def add_into(dst, src, n):
        def body(i, carry):
            dst[i] = (dst[i].astype(jnp.float32) + src[i].astype(jnp.float32)).astype(jnp.bfloat16)
            return carry

        lax.fori_loop(0, n, body, 0)

    def products(which, lo, hi, left, base, back):
        dims = (((1,), (1,)), ((), ())) if back else (((1,), (0,)), ((), ()))
        unroll = 8

        def body(i, acc):
            for u in range(unroll):
                j = lo + i * unroll + u
                v = lists[which, j]
                prod = lax.dot_general(
                    left[(v >> 9) & 127], wb[v & 511], dims, preferred_element_type=jnp.float32
                )
                acc = acc * (v >> 16).astype(jnp.float32) + prod
                sums[base + j] = acc
            return acc

        return lambda acc: lax.fori_loop(0, (hi - lo) // unroll, body, acc)

    zero = jnp.zeros((B, B), jnp.float32)

    def gather_blocks(which, dst):
        def body(i, carry):
            dst[i] = sums[lasts[which, i]].astype(jnp.bfloat16)
            return carry

        lax.fori_loop(0, DB, body, 0, unroll=4)

    def slot_grads(k, parity, left, right, left_hidden, row_base):
        def body(b, carry):
            s0 = ((b % 2) * 8 + (b // 2) * 2 + parity) * 6
            for u in range(6):
                v = pairs[k, s0 + u]
                f, h = v & 255, v >> 8
                i, j = (h, f) if left_hidden else (f, h + row_base)
                g = lax.dot_general(
                    left[i], right[j], (((0,), (0,)), ((), ())), preferred_element_type=jnp.float32
                )
                grads[parity, k * 48 + b * 6 + u] = g.astype(jnp.bfloat16)
            return carry

        lax.fori_loop(0, 8, body, 0)

    def core_piece(k, n):
        x = (px + (2, 1, 3, 0)[n]) % 4
        at = pl.ds(k * 48 + x * 12, 12)
        return remote(grads.at[1 - core, at], core_in.at[at], R_CORE + k * 4 + n, dev_core), at

    def core_send(k):
        for n in range(4):
            send(core_piece(k, n)[0])

    def core_add(k, n):
        copy, at = core_piece(k, n)
        copy.wait_recv()
        add_into(grads.at[core, at], core_in.at[at], 12)

    def reduce_grads(k):
        part = lambda j, r: grads.at[core, pl.ds(k * 48 + r * 12 + j * 6, 6)]
        return Reduce(
            part, px, yh, dev_xp, dev_xm, dev_yh, ra_g.at[k], rb_g.at[k], rm_g.at[k], R_G + 7 * k
        )

    def reduce_rows(buf, which, base):
        part = lambda j, r: buf.at[pl.ds((r * 2 + j) * 8, 8)]
        return Reduce(
            part, z, yl, dev_zp, dev_zm, dev_yl, ra_o.at[which], rb_o.at[which], rm_o.at[which], base
        )

    gx, gg = Gather(xb, R_X), Gather(gb, R_OG)
    for i in range(8):
        local(inputs.at[:, pl.ds(i * B, B)], xb.at[t * 8 + i], L_X + i).wait()
    send(gx.a)
    send(gx.bp)
    send(gx.bm)
    for i in range(8):
        local(out_grad.at[:, pl.ds(i * B, B)], gb.at[t * 8 + i], L_OG + i).wait()
    send(gg.a)
    gx.a.wait_recv()
    send(gx.cp)
    send(gx.cm)
    gx.bp.wait_recv()
    send(gx.dp)
    gx.bm.wait_recv()
    send(gx.dm)
    send(gg.bp)
    send(gg.bm)
    gx.dp.wait_recv()
    gx.dm.wait_recv()
    send(gx.e)
    gg.a.wait_recv()
    send(gg.cp)
    send(gg.cm)
    for k in range(3):
        local(weights.at[k], wb.at[pl.ds(k * CAP, CAP)], L_W + k).wait()
    gx.cp.wait_recv()
    gx.cm.wait_recv()
    gx.e.wait_recv()

    products(0, 0, CAP, xb, 0, False)(zero)
    gg.bp.wait_recv()
    send(gg.dp)
    gg.bm.wait_recv()
    send(gg.dm)
    products(1, 0, CAP, xb, CAP, False)(zero)

    def forward(h, carry):
        g, u = sums[lasts[0, h]], sums[lasts[1, h]]
        gate[h], up[h] = g, u
        hidden[h] = (g * jax.nn.sigmoid(g) * u).astype(jnp.bfloat16)
        return carry

    lax.fori_loop(0, HB, forward, 0)
    gg.dp.wait_recv()
    gg.dm.wait_recv()
    send(gg.e)

    products(3, 0, CAP, hidden, 0, False)(zero)
    gather_blocks(3, ob)
    red_o = reduce_rows(ob, 0, R_O)
    red_o.start()
    gg.cp.wait_recv()
    gg.cm.wait_recv()
    gg.e.wait_recv()

    slot_grads(2, 1 - core, hidden, gb, True, 0)
    core_send(2)
    slot_grads(2, core, hidden, gb, True, 0)
    red_g = [reduce_grads(k) for k in range(3)]
    for n in range(3):
        core_add(2, n)
    red_g[2].start()
    core_add(2, 3)
    products(2, 0, CAP, gb, CAP, True)(zero)

    def backward(h, carry):
        g, u, hg = gate[h], up[h], sums[lasts[2, h]]
        sig = jax.nn.sigmoid(g)
        rows[h] = (hg * u * sig * (1.0 + g * (1.0 - sig))).astype(jnp.bfloat16)
        rows[h + HB] = (hg * (g * sig)).astype(jnp.bfloat16)
        return carry

    lax.fori_loop(0, HB, backward, 0)
    red_o.relay()
    slot_grads(0, 1 - core, xb, rows, False, 0)
    core_send(0)
    red_g[2].relay()
    slot_grads(0, core, xb, rows, False, 0)
    for n in range(3):
        core_add(0, n)
    red_g[0].start()
    core_add(0, 3)
    slot_grads(1, 1 - core, xb, rows, False, HB)
    core_send(1)
    slot_grads(1, core, xb, rows, False, HB)
    red_o.cross()
    red_g[0].relay()
    for n in range(3):
        core_add(1, n)
    red_g[1].start()
    core_add(1, 3)
    red_g[2].cross()
    products(4, 0, 2 * CAP, rows, 0, True)(zero)
    gather_blocks(4, ib)
    red_i = reduce_rows(ib, 1, R_I)
    red_i.start()
    red_g[1].relay()
    red_o.m.wait_recv()

    def finish_rows(red, out):
        for i in range(8):
            out[:, i * B : (i + 1) * B] = red.total(i).astype(jnp.bfloat16)

    finish_rows(red_o, out_o)

    def finish_grads(k):
        red = red_g[k]
        red.m.wait_recv()
        count = counts[0, k]

        def body(i, carry):
            g = red.total(i)
            alive = (d * 6 + i < count).astype(jnp.float32)
            m = 0.9 * mom[0, k, i] + 0.1 * g
            v = 0.95 * mom[1, k, i] + 0.05 * g * g
            out_u[k, i] = alive * m / (jnp.sqrt(v) + EPSILON)
            return carry

        lax.fori_loop(0, 6, body, 0)

    local(first, mom.at[0], L_M).wait()
    local(second, mom.at[1], L_M + 1).wait()
    finish_grads(2)
    red_i.relay()
    red_g[0].cross()
    red_i.cross()
    finish_grads(0)
    red_i.m.wait_recv()
    finish_rows(red_i, out_i)
    red_g[1].cross()
    finish_grads(1)
    for copy in sent:
        copy.wait_send()


def local_step(inputs, out_grad, weights, block_index, block_counts, first_moment, second_moment):
    lists, lasts, pairs = slot_lists(block_index, block_counts)
    any_, smem, vmem = (
        pl.BlockSpec(memory_space=s) for s in (pl.ANY, pltpu.SMEM, pltpu.VMEM)
    )
    f32, bf16 = jnp.float32, jnp.bfloat16
    blocks = lambda *n, dtype=bf16: pltpu.VMEM((*n, B, B), dtype)
    dma = pltpu.SemaphoreType.DMA
    return pl.pallas_call(
        kernel,
        out_shape=(
            jax.ShapeDtypeStruct(inputs.shape, bf16),
            jax.ShapeDtypeStruct(inputs.shape, bf16),
            jax.ShapeDtypeStruct(first_moment.shape, f32),
        ),
        in_specs=[any_, any_, any_, smem, smem, smem, smem, any_, any_],
        out_specs=[vmem, vmem, vmem],
        scratch_shapes=[
            blocks(DB),
            blocks(DB),
            blocks(3 * CAP),
            blocks(ZERO + 1, dtype=f32),
            blocks(HB, dtype=f32),
            blocks(HB, dtype=f32),
            blocks(HB),
            blocks(2 * HB),
            blocks(DB),
            blocks(DB),
            blocks(2, 3 * 48),
            blocks(3 * 48),
            blocks(2, 2, 8),
            blocks(2, 2, 2, 8),
            blocks(2, 8),
            blocks(3, 2, 6),
            blocks(3, 2, 2, 6),
            blocks(3, 6),
            blocks(2, 3, 6, dtype=f32),
            dma((N_LOCAL,)),
            dma((N_REMOTE,)),
            dma((N_REMOTE,)),
        ],
        compiler_params=pltpu.CompilerParams(
            collective_id=0, has_side_effects=True, vmem_limit_bytes=63_000_000
        ),
    )(inputs, out_grad, weights, lists, lasts, pairs, block_counts, first_moment, second_moment)


def solution(mesh):
    in_specs = (
        P("dp", "tensor"),
        P("dp", "tensor"),
        P(None, "tensor", None, None),
        P(None, "tensor", None),
        P("tensor", None),
        P(None, ("tensor", "dp"), None, None),
        P(None, ("tensor", "dp"), None, None),
    )
    out_specs = (P("dp", "tensor"), P("dp", "tensor"), P(None, ("tensor", "dp"), None, None))
    return jax.shard_map(local_step, mesh=mesh, in_specs=in_specs, out_specs=out_specs, check_vma=False)
```

```python
import functools

import jax
import jax.numpy as jnp
from jax import lax
from jax.experimental import pallas as pl
from jax.experimental.pallas import tpu as pltpu
from jax.sharding import PartitionSpec as P

MESH = pl.DeviceIdType.MESH
EPSILON = 1e-08
HB = 14
CAP = 96
DB = 64
B = 128
PAIRS = (56, 56, 56, 80, 128)
BASE = (0, 64, 64, 0, 0)
ZERO = 128
NO_SLOT = 3 * CAP

L_X, L_OG, L_W, L_M, L_IDX, L_LIST = 0, 8, 16, 19, 21, 23
N_LOCAL = 25
R_X, R_OG, R_O, R_I, R_GA, R_GB, R_CORE = 0, 8, 16, 23, 30, 51, 66
N_REMOTE = 84


def kernel(
    inputs, out_grad, weights, index, counts, first, second,
    out_o, out_i, out_u,
    xb, gb, wb, sums, gate, up, hidden, rows, ob, ib, grads, core_in,
    ra_o, rb_o, rm_o, ra_g, rb_g, rm_g, ya_g, yr_g, yb_g, mom,
    index_v, pairs, lists_v, lists,
    lsem, ssem, rsem,
):
    d, t = lax.axis_index("dp"), lax.axis_index("tensor")
    core, px, yh = d % 2, (d // 2) % 4, d // 8
    z, yl = t // 2, t % 2
    dev_core = (d + 1 - 2 * core, t)
    dev_xp = (yh * 8 + ((px + 1) % 4) * 2 + core, t)
    dev_xm = (yh * 8 + ((px + 3) % 4) * 2 + core, t)
    dev_yh = ((1 - yh) * 8 + px * 2 + core, t)
    dev_zp = (d, ((z + 1) % 4) * 2 + yl)
    dev_zm = (d, ((z + 3) % 4) * 2 + yl)
    dev_yl = (d, t + 1 - 2 * yl)

    def local(src, dst, sem):
        return pltpu.make_async_copy(src, dst, lsem.at[sem])

    def remote(src, dst, sem, dev):
        return pltpu.make_async_remote_copy(
            src_ref=src, dst_ref=dst, send_sem=ssem.at[sem], recv_sem=rsem.at[sem],
            device_id=dev, device_id_type=MESH,
        )

    sent = []

    def send(copy):
        copy.start()
        sent.append(copy)

    for i in range(8):
        local(inputs.at[:, pl.ds(i * B, B)], xb.at[t * 8 + i], L_X + i).start()
    for i in range(8):
        local(out_grad.at[:, pl.ds(i * B, B)], gb.at[t * 8 + i], L_OG + i).start()
    barrier = pltpu.get_barrier_semaphore()
    for dev in (dev_core, dev_xp, dev_xm, dev_yh, dev_zp, dev_zm, dev_yl):
        pl.semaphore_signal(barrier, inc=1, device_id=dev, device_id_type=MESH)
    for k in range(3):
        local(weights.at[k], wb.at[pl.ds(k * CAP, CAP)], L_W + k).start()
    local(first, mom.at[0], L_M).start()
    local(second, mom.at[1], L_M + 1).start()
    local(index, index_v, L_IDX).start()
    local(index, pairs, L_IDX + 1).start()
    wb[NO_SLOT] = jnp.zeros((B, B), jnp.bfloat16)
    sums[ZERO] = jnp.zeros((B, B), jnp.float32)
    pl.semaphore_wait(barrier, 7)

    class Gather:
        def __init__(self, buf, base):
            chunk = lambda zz, yy, lo=0, n=8: buf.at[pl.ds((((zz + 4) % 4) * 2 + yy) * 8 + lo, n)]
            mk = lambda ref, sem, dev: remote(ref, ref, base + sem, dev)
            other = 1 - yl
            self.a = mk(chunk(z, yl), 0, dev_yl)
            self.bp = mk(chunk(z, yl), 1, dev_zp)
            self.bm = mk(chunk(z, yl), 2, dev_zm)
            self.cp = mk(chunk(z, other), 3, dev_zp)
            self.cm = mk(chunk(z, other), 4, dev_zm)
            self.dp = mk(chunk(z - 1, yl, 0, 4), 5, dev_zp)
            self.dm = mk(chunk(z + 1, yl, 4, 4), 6, dev_zm)
            self.e = mk(chunk(z + 2, yl), 7, dev_yl)

    class Reduce:
        def __init__(self, part, pos, pair, dev_p, dev_m, dev_pair, ra, rb, rm, base):
            nxt, opp, prv = (pos + 1) % 4, (pos + 2) % 4, (pos + 3) % 4
            self.part, self.pos, self.pair = part, pos, pair
            self.nxt, self.prv = nxt, prv
            self.ra, self.rb, self.rm = ra, rb, rm
            self.ap = remote(part(0, opp), ra.at[0], base, dev_p)
            self.am = remote(part(1, opp), ra.at[1], base + 1, dev_m)
            self.bp0 = remote(part(0, nxt), rb.at[0, 0], base + 2, dev_p)
            self.bp1 = remote(part(1, nxt), rb.at[0, 1], base + 3, dev_p)
            self.bm0 = remote(part(0, prv), rb.at[1, 0], base + 4, dev_m)
            self.bm1 = remote(part(1, prv), rb.at[1, 1], base + 5, dev_m)
            self.m = remote(part(1 - pair, pos), rm, base + 6, dev_pair)
            self.n = rm.shape[0]

        def start(self):
            send(self.ap)
            send(self.am)

        def more(self):
            send(self.bp1)
            send(self.bm0)

        def relay(self):
            self.ap.wait_recv()
            add_into(self.part(0, self.nxt), self.ra.at[0], self.n)
            send(self.bp0)
            self.am.wait_recv()
            add_into(self.part(1, self.prv), self.ra.at[1], self.n)
            send(self.bm1)

        def cross(self):
            for b in (self.bp0, self.bp1, self.bm0, self.bm1):
                b.wait_recv()
            far = 1 - self.pair
            mine = self.part(far, self.pos)

            def body(i, carry):
                v = mine[i].astype(jnp.float32) + self.rb[0, far, i].astype(jnp.float32)
                mine[i] = (v + self.rb[1, far, i].astype(jnp.float32)).astype(jnp.bfloat16)
                return carry

            lax.fori_loop(0, self.n, body, 0)
            send(self.m)

        def total(self, i):
            mine = self.part(self.pair, self.pos)
            v = mine[i].astype(jnp.float32) + self.rb[0, self.pair, i].astype(jnp.float32)
            v = v + self.rb[1, self.pair, i].astype(jnp.float32)
            return v + self.rm[i].astype(jnp.float32)

    def add_into(dst, src, n):
        def body(i, carry):
            dst[i] = (dst[i].astype(jnp.float32) + src[i].astype(jnp.float32)).astype(jnp.bfloat16)
            return carry

        lax.fori_loop(0, n, body, 0)

    def products(which, lo, hi, left, back):
        dims = (((1,), (1,)), ((), ())) if back else (((1,), (0,)), ((), ()))
        unroll, base = 8, BASE[which]

        def body(i, acc):
            for u in range(unroll):
                j = lo + i * unroll + u
                v, w = lists[which, 2 * j], lists[which, 2 * j + 1]
                prod = lax.dot_general(
                    jnp.concatenate([left[(v >> 9) & 127], left[(w >> 9) & 127]], axis=1),
                    jnp.concatenate([wb[v & 511], wb[w & 511]], axis=1 if back else 0),
                    dims,
                    preferred_element_type=jnp.float32,
                )
                acc = acc * (v >> 16).astype(jnp.float32) + prod
                sums[base + j] = acc
            return acc

        return lambda acc: lax.fori_loop(0, (hi - lo) // unroll, body, acc)

    zero = jnp.zeros((B, B), jnp.float32)

    def gather_blocks(which, dst):
        def body(i, carry):
            dst[i] = sums[lists[5 + which, i]].astype(jnp.bfloat16)
            return carry

        lax.fori_loop(0, DB, body, 0, unroll=4)

    def slot_grads(k, parity, left, right, left_hidden, row_base):
        def body(b, carry):
            x, y = b // 2, b % 2
            s0 = (y * 8 + x * 2 + parity) * 6
            for u in range(6):
                f, h = pairs[k, 0, s0 + u], pairs[k, 1, s0 + u]
                i, j = (h, f) if left_hidden else (f, h + row_base)
                g = lax.dot_general(
                    left[i], right[j], (((0,), (0,)), ((), ())), preferred_element_type=jnp.float32
                )
                at = b * 4 + u if u < 4 else 28 + (y * 4 + x) * 2 + u
                grads[parity, k * 48 + at] = g.astype(jnp.bfloat16)
            return carry

        lax.fori_loop(0, 8, body, 0)

    def core_piece(k, n):
        nxt, opp, prv = (px + 1) % 4, (px + 2) % 4, (px + 3) % 4
        first_block = (opp * 8, 32 + (1 - yh) * 8, nxt * 8, prv * 8, 32 + yh * 8, px * 8)[n]
        at = pl.ds(k * 48 + first_block, 8)
        return remote(grads.at[1 - core, at], core_in.at[at], R_CORE + k * 6 + n, dev_core), at

    def core_send(k):
        for n in range(6):
            send(core_piece(k, n)[0])

    def core_add(k, n):
        copy, at = core_piece(k, n)
        copy.wait_recv()
        add_into(grads.at[core, at], core_in.at[at], 8)

    def reduce_grads(k):
        part = lambda j, r: grads.at[core, pl.ds(k * 48 + (r * 2 + j) * 4, 4)]
        return Reduce(
            part, px, yh, dev_xp, dev_xm, dev_yh, ra_g.at[k], rb_g.at[k], rm_g.at[k], R_GA + 7 * k
        )

    class PairFirst:
        def __init__(self, k):
            nxt, opp, prv = (px + 1) % 4, (px + 2) % 4, (px + 3) % 4
            at = lambda y, x, j, n: grads.at[core, pl.ds(k * 48 + 32 + (y * 4 + x) * 2 + j, n)]
            base = R_GB + 5 * k
            self.mine, self.got = at(yh, 0, 0, 8), ya_g.at[k]
            self.y = remote(at(1 - yh, 0, 0, 8), ya_g.at[k], base, dev_yh)
            self.ap = remote(at(yh, opp, 0, 1), yr_g.at[k, 0], base + 1, dev_xp)
            self.am = remote(at(yh, opp, 1, 1), yr_g.at[k, 1], base + 2, dev_xm)
            self.bp = remote(at(yh, nxt, 0, 2), yb_g.at[k, 0], base + 3, dev_xp)
            self.bm = remote(at(yh, prv, 0, 2), yb_g.at[k, 1], base + 4, dev_xm)
            self.for_p, self.for_m, self.last = at(yh, nxt, 0, 1), at(yh, prv, 1, 1), at(yh, px, 0, 2)
            self.relayed, self.ends = yr_g.at[k], yb_g.at[k]

        def ring(self):
            self.y.wait_recv()
            add_into(self.mine, self.got, 8)
            send(self.ap)
            send(self.am)

        def relay(self):
            self.ap.wait_recv()
            add_into(self.for_p, self.relayed.at[0], 1)
            send(self.bp)
            self.am.wait_recv()
            add_into(self.for_m, self.relayed.at[1], 1)
            send(self.bm)

        def total(self, i):
            v = self.last[i].astype(jnp.float32) + self.ends[0, i].astype(jnp.float32)
            return v + self.ends[1, i].astype(jnp.float32)

    def reduce_rows(buf, which, base):
        part = lambda j, r: buf.at[pl.ds((r * 2 + j) * 8, 8)]
        return Reduce(
            part, z, yl, dev_zp, dev_zm, dev_yl, ra_o.at[which], rb_o.at[which], rm_o.at[which], base
        )

    def build_lists():
        n, wide = CAP, 2 * B
        row_i = lax.broadcasted_iota(jnp.int32, (n, n), 0)
        lane_i = lax.broadcasted_iota(jnp.int32, (n, n), 1)
        eye = row_i == lane_i
        earlier = lane_i < row_i
        later = lane_i > row_i
        lane1 = lax.broadcasted_iota(jnp.int32, (1, n), 1)
        place = lax.broadcasted_iota(jnp.int32, (n, wide), 1)
        group = lax.broadcasted_iota(jnp.int32, (n, wide), 1)

        def flag(m):
            return jnp.where(m, 1, 0)

        def spread(row):
            return jnp.broadcast_to(row, (n, n))

        def column(row):
            return jnp.sum(jnp.where(eye, spread(row), 0), axis=1, keepdims=True)

        def items(k, target, source, source_base):
            alive = lane1 < counts[0, k]
            key = jnp.where(alive, index_v[k, target : target + 1, :], DB)
            src = index_v[k, source : source + 1, :] + source_base
            return key, lane1 + k * CAP + (src << 9)

        def one_list(which, sets):
            keys = [key for key, _ in sets]
            cols = [column(key) for key in keys]
            m = len(sets)
            odd_last = []
            for b in range(m):
                same = [flag(cols[a] == spread(keys[b])) for a in range(m)]
                count = sum(jnp.sum(s, axis=0, keepdims=True) for s in same)
                rank = jnp.sum(jnp.where(later, same[b], 0), axis=0, keepdims=True)
                for a in range(b):
                    rank = rank + jnp.sum(same[a], axis=0, keepdims=True)
                odd_last.append(jnp.where(rank + 1 == count, count & 1, 0))
            filled = jnp.zeros((1, wide), jnp.int32)
            taken = jnp.zeros((1, wide), jnp.int32)
            last = jnp.full((1, wide), -1, jnp.int32)
            for a in range(m):
                before = jnp.zeros((n, 1), jnp.int32)
                rank = jnp.zeros((n, 1), jnp.int32)
                for b in range(m):
                    less = spread(keys[b]) < cols[a]
                    weight = spread(1 + odd_last[b])
                    before = before + jnp.sum(jnp.where(less, weight, 0), axis=1, keepdims=True)
                    same = flag(spread(keys[b]) == cols[a])
                    if b == a:
                        same = jnp.where(earlier, same, 0)
                    if b <= a:
                        rank = rank + jnp.sum(same, axis=1, keepdims=True)
                at = before + rank
                packed = column(sets[a][1]) + jnp.where(rank >= 2, 65536, 0)
                hit = at == place
                filled = filled + jnp.sum(jnp.where(hit, packed, 0), axis=0, keepdims=True)
                taken = taken + jnp.sum(flag(hit), axis=0, keepdims=True)
                step = at >> 1
                mine = jnp.where(cols[a] == group, step, -1)
                last = jnp.maximum(last, jnp.max(mine, axis=0, keepdims=True))
            entry = jnp.where(taken > 0, filled, NO_SLOT)
            lists_v[which : which + 1, :] = entry
            last = jnp.where(last < 0, ZERO, last + BASE[which])
            lists_v[5 + which : 6 + which, :] = last

        local(index, index_v, L_IDX).wait()
        one_list(0, [items(0, 1, 0, 0)])
        one_list(1, [items(1, 1, 0, 0)])
        one_list(2, [items(2, 1, 0, 0)])
        one_list(3, [items(2, 0, 1, 0)])
        one_list(4, [items(0, 0, 1, 0), items(1, 0, 1, HB)])
        copy = local(lists_v, lists, L_LIST)
        copy.start()
        copy.wait()
        local(index, pairs, L_IDX + 1).wait()

    gx, gg = Gather(xb, R_X), Gather(gb, R_OG)
    for i in range(8):
        local(inputs.at[:, pl.ds(i * B, B)], xb.at[t * 8 + i], L_X + i).wait()
    send(gx.bp)
    send(gx.bm)
    send(gx.a)
    for i in range(8):
        local(out_grad.at[:, pl.ds(i * B, B)], gb.at[t * 8 + i], L_OG + i).wait()
    send(gg.bp)
    send(gg.bm)
    send(gg.a)
    build_lists()
    gx.bp.wait_recv()
    send(gx.dp)
    gx.bm.wait_recv()
    send(gx.dm)
    gx.a.wait_recv()
    send(gx.cp)
    send(gx.cm)
    gg.bp.wait_recv()
    send(gg.dp)
    gg.bm.wait_recv()
    send(gg.dm)
    gg.a.wait_recv()
    send(gg.cp)
    send(gg.cm)
    gx.dp.wait_recv()
    gx.dm.wait_recv()
    send(gx.e)
    for k in range(3):
        local(weights.at[k], wb.at[pl.ds(k * CAP, CAP)], L_W + k).wait()
    gx.cp.wait_recv()
    gx.cm.wait_recv()
    gx.e.wait_recv()

    acc = products(0, 0, 32, xb, False)(zero)
    gg.dp.wait_recv()
    gg.dm.wait_recv()
    send(gg.e)
    products(0, 32, PAIRS[0], xb, False)(acc)
    products(1, 0, PAIRS[1], xb, False)(zero)

    def forward(h, carry):
        g, u = sums[lists[5, h]], sums[lists[6, h]]
        gate[h], up[h] = g, u
        hidden[h] = (g * jax.nn.sigmoid(g) * u).astype(jnp.bfloat16)
        return carry

    lax.fori_loop(0, HB, forward, 0)

    products(3, 0, PAIRS[3], hidden, False)(zero)
    gather_blocks(3, ob)
    red_o = reduce_rows(ob, 0, R_O)
    red_o.start()
    red_o.more()
    gg.cp.wait_recv()
    gg.cm.wait_recv()
    gg.e.wait_recv()

    red_g = [reduce_grads(k) for k in range(3)]
    red_y = [PairFirst(k) for k in range(3)]

    def start_grads(k):
        core_add(k, 0)
        red_g[k].start()
        core_add(k, 1)
        send(red_y[k].y)
        core_add(k, 2)
        core_add(k, 3)
        red_g[k].more()
        core_add(k, 4)
        core_add(k, 5)

    slot_grads(2, 1 - core, hidden, gb, True, 0)
    core_send(2)
    slot_grads(2, core, hidden, gb, True, 0)
    start_grads(2)
    products(2, 0, PAIRS[2], gb, True)(zero)

    def backward(h, carry):
        g, u, hg = gate[h], up[h], sums[lists[7, h]]
        sig = jax.nn.sigmoid(g)
        rows[h] = (hg * u * sig * (1.0 + g * (1.0 - sig))).astype(jnp.bfloat16)
        rows[h + HB] = (hg * (g * sig)).astype(jnp.bfloat16)
        return carry

    lax.fori_loop(0, HB, backward, 0)
    red_o.relay()
    slot_grads(0, 1 - core, xb, rows, False, 0)
    core_send(0)
    red_g[2].relay()
    slot_grads(0, core, xb, rows, False, 0)
    red_y[2].ring()
    start_grads(0)
    acc = products(4, 0, 64, rows, True)(zero)
    red_y[2].relay()
    red_o.cross()
    products(4, 64, PAIRS[4], rows, True)(acc)
    gather_blocks(4, ib)
    red_i = reduce_rows(ib, 1, R_I)
    red_i.start()
    red_i.more()
    red_g[0].relay()
    red_g[2].cross()
    slot_grads(1, 1 - core, xb, rows, False, HB)
    core_send(1)
    red_y[0].ring()
    slot_grads(1, core, xb, rows, False, HB)
    start_grads(1)
    red_i.relay()
    red_o.m.wait_recv()

    def finish_rows(red, out):
        for i in range(8):
            out[:, i * B : (i + 1) * B] = red.total(i).astype(jnp.bfloat16)

    finish_rows(red_o, out_o)

    def finish_grads(k):
        red = red_g[k]
        count = counts[0, k]

        def update(source, shift, i, carry):
            g = source.total(i)
            i = i + shift
            alive = (d * 6 + i < count).astype(jnp.float32)
            m = 0.9 * mom[0, k, i] + 0.1 * g
            v = 0.95 * mom[1, k, i] + 0.05 * g * g
            out_u[k, i] = alive * m / (jnp.sqrt(v) + EPSILON)
            return carry

        lax.fori_loop(0, 2, functools.partial(update, red_y[k], 4), 0)
        red.m.wait_recv()
        lax.fori_loop(0, 4, functools.partial(update, red, 0), 0)

    def end_pair_first(k):
        red_y[k].bp.wait_recv()
        red_y[k].bm.wait_recv()

    local(first, mom.at[0], L_M).wait()
    local(second, mom.at[1], L_M + 1).wait()
    red_y[0].relay()
    end_pair_first(2)
    finish_grads(2)
    red_g[0].cross()
    red_g[1].relay()
    red_y[1].ring()
    red_i.cross()
    end_pair_first(0)
    finish_grads(0)
    red_y[1].relay()
    red_i.m.wait_recv()
    finish_rows(red_i, out_i)
    red_g[1].cross()
    end_pair_first(1)
    finish_grads(1)
    for copy in sent:
        copy.wait_send()


def store(*refs):
    src, dst, sem = refs[:3], refs[3:6], refs[6]
    copies = [pltpu.make_async_copy(s, o, sem.at[i]) for i, (s, o) in enumerate(zip(src, dst))]
    for copy in copies:
        copy.start()
    for copy in copies:
        copy.wait()


def local_step(inputs, out_grad, weights, block_index, block_counts, first_moment, second_moment):
    index = jnp.transpose(block_index, (0, 2, 1))
    any_, smem, vmem = (
        pl.BlockSpec(memory_space=s) for s in (pl.ANY, pltpu.SMEM, pltpu.VMEM)
    )
    f32, bf16, i32 = jnp.float32, jnp.bfloat16, jnp.int32
    blocks = lambda *n, dtype=bf16: pltpu.VMEM((*n, B, B), dtype)
    dma = pltpu.SemaphoreType.DMA
    shapes = (
        jax.ShapeDtypeStruct(inputs.shape, bf16),
        jax.ShapeDtypeStruct(inputs.shape, bf16),
        jax.ShapeDtypeStruct(first_moment.shape, f32),
    )
    results = pl.pallas_call(
        kernel,
        out_shape=shapes,
        in_specs=[any_, any_, any_, any_, smem, any_, any_],
        out_specs=[vmem, vmem, vmem],
        scratch_shapes=[
            blocks(DB),
            blocks(DB),
            blocks(3 * CAP + 1),
            blocks(ZERO + 1, dtype=f32),
            blocks(HB, dtype=f32),
            blocks(HB, dtype=f32),
            blocks(HB),
            blocks(2 * HB),
            blocks(DB),
            blocks(DB),
            blocks(2, 3 * 48),
            blocks(3 * 48),
            blocks(2, 2, 8),
            blocks(2, 2, 2, 8),
            blocks(2, 8),
            blocks(3, 2, 4),
            blocks(3, 2, 2, 4),
            blocks(3, 4),
            blocks(3, 8),
            blocks(3, 2, 1),
            blocks(3, 2, 2),
            blocks(2, 3, 6, dtype=f32),
            pltpu.VMEM((3, 2, CAP), i32),
            pltpu.SMEM((3, 2, CAP), i32),
            pltpu.VMEM((16, 2 * B), i32),
            pltpu.SMEM((16, 2 * B), i32),
            dma((N_LOCAL,)),
            dma((N_REMOTE,)),
            dma((N_REMOTE,)),
        ],
        compiler_params=pltpu.CompilerParams(
            collective_id=0, has_side_effects=True, vmem_limit_bytes=63_000_000
        ),
    )(inputs, out_grad, weights, index, block_counts, first_moment, second_moment)
    return pl.pallas_call(
        store,
        out_shape=shapes,
        in_specs=[vmem, vmem, vmem],
        out_specs=[any_, any_, any_],
        scratch_shapes=[dma((3,))],
    )(*results)


def solution(mesh):
    in_specs = (
        P("dp", "tensor"),
        P("dp", "tensor"),
        P(None, "tensor", None, None),
        P(None, "tensor", None),
        P("tensor", None),
        P(None, ("tensor", "dp"), None, None),
        P(None, ("tensor", "dp"), None, None),
    )
    out_specs = (P("dp", "tensor"), P("dp", "tensor"), P(None, ("tensor", "dp"), None, None))
    return jax.shard_map(local_step, mesh=mesh, in_specs=in_specs, out_specs=out_specs, check_vma=False)
```

```python
import functools

import jax
import jax.numpy as jnp
from jax import lax
from jax.experimental import pallas as pl
from jax.experimental.pallas import tpu as pltpu
from jax.sharding import PartitionSpec as P

MESH = pl.DeviceIdType.MESH
EPSILON = 1e-08
HB = 14
CAP = 96
DB = 64
B = 128
PAIRS = (56, 56, 56, 80, 128)
UNROLL = (28, 28, 28, 20, 32)
BASE = (0, 64, 64, 0, 0)
ZERO = 128
NO_SLOT = 3 * CAP

L_X, L_OG, L_W, L_M, L_IDX, L_LIST = 0, 8, 16, 19, 21, 23
N_LOCAL = 25
R_X, R_OG, R_O, R_I, R_GA, R_GB, R_CORE = 0, 8, 16, 23, 30, 51, 66
N_REMOTE = 84


def kernel(
    inputs, out_grad, weights, index, counts, first, second,
    out_o, out_i, out_u,
    xb, gb, wb, sums, gate, up, hidden, rows, ob, ib, grads, core_in,
    ra_o, rb_o, rm_o, ra_g, rb_g, rm_g, ya_g, yr_g, yb_g, mom,
    index_v, pairs, lists_v, lists,
    lsem, ssem, rsem,
):
    d, t = lax.axis_index("dp"), lax.axis_index("tensor")
    core, px, yh = d % 2, (d // 2) % 4, d // 8
    z, yl = t // 2, t % 2
    dev_core = (d + 1 - 2 * core, t)
    dev_xp = (yh * 8 + ((px + 1) % 4) * 2 + core, t)
    dev_xm = (yh * 8 + ((px + 3) % 4) * 2 + core, t)
    dev_yh = ((1 - yh) * 8 + px * 2 + core, t)
    dev_zp = (d, ((z + 1) % 4) * 2 + yl)
    dev_zm = (d, ((z + 3) % 4) * 2 + yl)
    dev_yl = (d, t + 1 - 2 * yl)

    def local(src, dst, sem):
        return pltpu.make_async_copy(src, dst, lsem.at[sem])

    def remote(src, dst, sem, dev):
        return pltpu.make_async_remote_copy(
            src_ref=src, dst_ref=dst, send_sem=ssem.at[sem], recv_sem=rsem.at[sem],
            device_id=dev, device_id_type=MESH,
        )

    sent = []

    def send(copy):
        copy.start()
        sent.append(copy)

    for i in range(8):
        local(inputs.at[:, pl.ds(i * B, B)], xb.at[t * 8 + i], L_X + i).start()
    for i in range(8):
        local(out_grad.at[:, pl.ds(i * B, B)], gb.at[t * 8 + i], L_OG + i).start()
    barrier = pltpu.get_barrier_semaphore()
    for dev in (dev_core, dev_xp, dev_xm, dev_yh, dev_zp, dev_zm, dev_yl):
        pl.semaphore_signal(barrier, inc=1, device_id=dev, device_id_type=MESH)
    local(index, index_v, L_IDX).start()
    local(index, pairs, L_IDX + 1).start()
    wb[NO_SLOT] = jnp.zeros((B, B), jnp.bfloat16)
    sums[ZERO] = jnp.zeros((B, B), jnp.float32)
    pl.semaphore_wait(barrier, 7)

    class Gather:
        def __init__(self, buf, base):
            chunk = lambda zz, yy, lo=0, n=8: buf.at[pl.ds((((zz + 4) % 4) * 2 + yy) * 8 + lo, n)]
            mk = lambda ref, sem, dev: remote(ref, ref, base + sem, dev)
            other = 1 - yl
            self.a = mk(chunk(z, yl), 0, dev_yl)
            self.bp = mk(chunk(z, yl), 1, dev_zp)
            self.bm = mk(chunk(z, yl), 2, dev_zm)
            self.cp = mk(chunk(z, other), 3, dev_zp)
            self.cm = mk(chunk(z, other), 4, dev_zm)
            self.dp = mk(chunk(z - 1, yl, 0, 4), 5, dev_zp)
            self.dm = mk(chunk(z + 1, yl, 4, 4), 6, dev_zm)
            self.e = mk(chunk(z + 2, yl), 7, dev_yl)

    class Reduce:
        def __init__(self, part, pos, pair, dev_p, dev_m, dev_pair, ra, rb, rm, base):
            nxt, opp, prv = (pos + 1) % 4, (pos + 2) % 4, (pos + 3) % 4
            self.part, self.pos, self.pair = part, pos, pair
            self.nxt, self.prv = nxt, prv
            self.ra, self.rb, self.rm = ra, rb, rm
            self.ap = remote(part(0, opp), ra.at[0], base, dev_p)
            self.am = remote(part(1, opp), ra.at[1], base + 1, dev_m)
            self.bp0 = remote(part(0, nxt), rb.at[0, 0], base + 2, dev_p)
            self.bp1 = remote(part(1, nxt), rb.at[0, 1], base + 3, dev_p)
            self.bm0 = remote(part(0, prv), rb.at[1, 0], base + 4, dev_m)
            self.bm1 = remote(part(1, prv), rb.at[1, 1], base + 5, dev_m)
            self.m = remote(part(1 - pair, pos), rm, base + 6, dev_pair)
            self.n = rm.shape[0]

        def start(self):
            send(self.ap)
            send(self.am)

        def more(self):
            send(self.bp1)
            send(self.bm0)

        def relay(self):
            self.ap.wait_recv()
            add_into(self.part(0, self.nxt), self.ra.at[0], self.n)
            send(self.bp0)
            self.am.wait_recv()
            add_into(self.part(1, self.prv), self.ra.at[1], self.n)
            send(self.bm1)

        def cross(self):
            for b in (self.bp0, self.bp1, self.bm0, self.bm1):
                b.wait_recv()
            far = 1 - self.pair
            mine = self.part(far, self.pos)

            for i in range(self.n):
                v = mine[i].astype(jnp.float32) + self.rb[0, far, i].astype(jnp.float32)
                mine[i] = (v + self.rb[1, far, i].astype(jnp.float32)).astype(jnp.bfloat16)
            send(self.m)

        def total(self, i):
            mine = self.part(self.pair, self.pos)
            v = mine[i].astype(jnp.float32) + self.rb[0, self.pair, i].astype(jnp.float32)
            v = v + self.rb[1, self.pair, i].astype(jnp.float32)
            return v + self.rm[i].astype(jnp.float32)

    def add_into(dst, src, n):
        for i in range(n):
            dst[i] = (dst[i].astype(jnp.float32) + src[i].astype(jnp.float32)).astype(jnp.bfloat16)

    def products(which, lo, hi, left, back):
        dims = (((1,), (1,)), ((), ())) if back else (((1,), (0,)), ((), ()))
        unroll, base = UNROLL[which], BASE[which]

        def body(i, acc):
            for u in range(unroll):
                j = lo + i * unroll + u
                v, w = lists[which, 2 * j], lists[which, 2 * j + 1]
                prod = lax.dot_general(
                    jnp.concatenate([left[(v >> 9) & 127], left[(w >> 9) & 127]], axis=1),
                    jnp.concatenate([wb[v & 511], wb[w & 511]], axis=1 if back else 0),
                    dims,
                    preferred_element_type=jnp.float32,
                )
                acc = acc * (v >> 16).astype(jnp.float32) + prod
                sums[base + j] = acc
            return acc

        return lambda acc: lax.fori_loop(0, (hi - lo) // unroll, body, acc)

    zero = jnp.zeros((B, B), jnp.float32)

    def gather_blocks(which, dst):
        def body(i, carry):
            dst[i] = sums[lists[5 + which, i]].astype(jnp.bfloat16)
            return carry

        lax.fori_loop(0, DB, body, 0, unroll=16)

    def piece_of(n):
        nxt, opp, prv = (px + 1) % 4, (px + 2) % 4, (px + 3) % 4
        ring = (opp, None, nxt, prv, None, px)[n]
        pair = (None, 1 - yh, None, None, yh, None)[n]
        return ring, pair, ring * 8 if pair is None else 32 + pair * 8

    def slot_grads(k, parity, pieces):
        left, right, left_hidden, row_base = (
            (xb, rows, False, 0), (xb, rows, False, HB), (hidden, gb, True, 0)
        )[k]
        for n in pieces:
            ring, pair, block = piece_of(n)
            for i in range(8):
                if pair is None:
                    slot = ((i // 4) * 8 + ring * 2 + parity) * 6 + i % 4
                else:
                    slot = (pair * 8 + (i // 2) * 2 + parity) * 6 + 4 + i % 2
                f, h = pairs[k, 0, slot], pairs[k, 1, slot]
                li, ri = (h, f) if left_hidden else (f, h + row_base)
                g = lax.dot_general(
                    left[li], right[ri], (((0,), (0,)), ((), ())), preferred_element_type=jnp.float32
                )
                grads[parity, k * 48 + block + i] = g.astype(jnp.bfloat16)

    def core_piece(k, n):
        at = pl.ds(k * 48 + piece_of(n)[2], 8)
        return remote(grads.at[1 - core, at], core_in.at[at], R_CORE + k * 6 + n, dev_core), at

    def core_send(k, pieces):
        for n in pieces:
            send(core_piece(k, n)[0])

    def core_add(k, n):
        copy, at = core_piece(k, n)
        copy.wait_recv()
        add_into(grads.at[core, at], core_in.at[at], 8)

    def reduce_grads(k):
        part = lambda j, r: grads.at[core, pl.ds(k * 48 + (r * 2 + j) * 4, 4)]
        return Reduce(
            part, px, yh, dev_xp, dev_xm, dev_yh, ra_g.at[k], rb_g.at[k], rm_g.at[k], R_GA + 7 * k
        )

    class PairFirst:
        def __init__(self, k):
            nxt, opp, prv = (px + 1) % 4, (px + 2) % 4, (px + 3) % 4
            at = lambda y, x, j, n: grads.at[core, pl.ds(k * 48 + 32 + (y * 4 + x) * 2 + j, n)]
            base = R_GB + 5 * k
            self.mine, self.got = at(yh, 0, 0, 8), ya_g.at[k]
            self.y = remote(at(1 - yh, 0, 0, 8), ya_g.at[k], base, dev_yh)
            self.ap = remote(at(yh, opp, 0, 1), yr_g.at[k, 0], base + 1, dev_xp)
            self.am = remote(at(yh, opp, 1, 1), yr_g.at[k, 1], base + 2, dev_xm)
            self.bp = remote(at(yh, nxt, 0, 2), yb_g.at[k, 0], base + 3, dev_xp)
            self.bm = remote(at(yh, prv, 0, 2), yb_g.at[k, 1], base + 4, dev_xm)
            self.for_p, self.for_m, self.last = at(yh, nxt, 0, 1), at(yh, prv, 1, 1), at(yh, px, 0, 2)
            self.relayed, self.ends = yr_g.at[k], yb_g.at[k]

        def ring(self):
            self.y.wait_recv()
            add_into(self.mine, self.got, 8)
            send(self.ap)
            send(self.am)

        def relay(self):
            self.ap.wait_recv()
            add_into(self.for_p, self.relayed.at[0], 1)
            send(self.bp)
            self.am.wait_recv()
            add_into(self.for_m, self.relayed.at[1], 1)
            send(self.bm)

        def total(self, i):
            v = self.last[i].astype(jnp.float32) + self.ends[0, i].astype(jnp.float32)
            return v + self.ends[1, i].astype(jnp.float32)

    def reduce_rows(buf, which, base):
        part = lambda j, r: buf.at[pl.ds((r * 2 + j) * 8, 8)]
        return Reduce(
            part, z, yl, dev_zp, dev_zm, dev_yl, ra_o.at[which], rb_o.at[which], rm_o.at[which], base
        )

    def build_lists():
        n, wide = CAP, 2 * B
        row_i = lax.broadcasted_iota(jnp.int32, (n, n), 0)
        lane_i = lax.broadcasted_iota(jnp.int32, (n, n), 1)
        eye = row_i == lane_i
        earlier = lane_i < row_i
        later = lane_i > row_i
        lane1 = lax.broadcasted_iota(jnp.int32, (1, n), 1)
        place = lax.broadcasted_iota(jnp.int32, (n, wide), 1)
        group = lax.broadcasted_iota(jnp.int32, (n, wide), 1)

        def flag(m):
            return jnp.where(m, 1, 0)

        def spread(row):
            return jnp.broadcast_to(row, (n, n))

        def column(row):
            return jnp.sum(jnp.where(eye, spread(row), 0), axis=1, keepdims=True)

        def items(k, target, source, source_base):
            alive = lane1 < counts[0, k]
            key = jnp.where(alive, index_v[k, target : target + 1, :], DB)
            src = index_v[k, source : source + 1, :] + source_base
            return key, lane1 + k * CAP + (src << 9)

        def one_list(which, sets):
            keys = [key for key, _ in sets]
            cols = [column(key) for key in keys]
            m = len(sets)
            odd_last = []
            for b in range(m):
                same = [flag(cols[a] == spread(keys[b])) for a in range(m)]
                count = sum(jnp.sum(s, axis=0, keepdims=True) for s in same)
                rank = jnp.sum(jnp.where(later, same[b], 0), axis=0, keepdims=True)
                for a in range(b):
                    rank = rank + jnp.sum(same[a], axis=0, keepdims=True)
                odd_last.append(jnp.where(rank + 1 == count, count & 1, 0))
            filled = jnp.zeros((1, wide), jnp.int32)
            taken = jnp.zeros((1, wide), jnp.int32)
            last = jnp.full((1, wide), -1, jnp.int32)
            for a in range(m):
                before = jnp.zeros((n, 1), jnp.int32)
                rank = jnp.zeros((n, 1), jnp.int32)
                for b in range(m):
                    less = spread(keys[b]) < cols[a]
                    weight = spread(1 + odd_last[b])
                    before = before + jnp.sum(jnp.where(less, weight, 0), axis=1, keepdims=True)
                    same = flag(spread(keys[b]) == cols[a])
                    if b == a:
                        same = jnp.where(earlier, same, 0)
                    if b <= a:
                        rank = rank + jnp.sum(same, axis=1, keepdims=True)
                at = before + rank
                packed = column(sets[a][1]) + jnp.where(rank >= 2, 65536, 0)
                hit = at == place
                filled = filled + jnp.sum(jnp.where(hit, packed, 0), axis=0, keepdims=True)
                taken = taken + jnp.sum(flag(hit), axis=0, keepdims=True)
                step = at >> 1
                mine = jnp.where(cols[a] == group, step, -1)
                last = jnp.maximum(last, jnp.max(mine, axis=0, keepdims=True))
            entry = jnp.where(taken > 0, filled, NO_SLOT)
            lists_v[which : which + 1, :] = entry
            last = jnp.where(last < 0, ZERO, last + BASE[which])
            lists_v[5 + which : 6 + which, :] = last

        local(index, index_v, L_IDX).wait()
        one_list(0, [items(0, 1, 0, 0)])
        one_list(1, [items(1, 1, 0, 0)])
        one_list(2, [items(2, 1, 0, 0)])
        one_list(3, [items(2, 0, 1, 0)])
        one_list(4, [items(0, 0, 1, 0), items(1, 0, 1, HB)])
        copy = local(lists_v, lists, L_LIST)
        copy.start()
        copy.wait()
        local(index, pairs, L_IDX + 1).wait()

    gx, gg = Gather(xb, R_X), Gather(gb, R_OG)
    for i in range(8):
        local(inputs.at[:, pl.ds(i * B, B)], xb.at[t * 8 + i], L_X + i).wait()
    send(gx.bp)
    send(gx.bm)
    send(gx.a)
    for i in range(8):
        local(out_grad.at[:, pl.ds(i * B, B)], gb.at[t * 8 + i], L_OG + i).wait()
    send(gg.bp)
    send(gg.bm)
    send(gg.a)
    for k in range(3):
        local(weights.at[k], wb.at[pl.ds(k * CAP, CAP)], L_W + k).start()
    local(first, mom.at[0], L_M).start()
    local(second, mom.at[1], L_M + 1).start()
    build_lists()
    gx.bp.wait_recv()
    send(gx.dp)
    gx.bm.wait_recv()
    send(gx.dm)
    gg.bp.wait_recv()
    send(gg.dp)
    gg.bm.wait_recv()
    send(gg.dm)
    gx.a.wait_recv()
    send(gx.cp)
    send(gx.cm)
    gg.a.wait_recv()
    send(gg.cp)
    send(gg.cm)
    gx.dp.wait_recv()
    gx.dm.wait_recv()
    send(gx.e)
    gg.dp.wait_recv()
    gg.dm.wait_recv()
    send(gg.e)
    for k in range(3):
        local(weights.at[k], wb.at[pl.ds(k * CAP, CAP)], L_W + k).wait()
    gx.cp.wait_recv()
    gx.cm.wait_recv()
    gx.e.wait_recv()

    products(0, 0, PAIRS[0], xb, False)(zero)
    products(1, 0, PAIRS[1], xb, False)(zero)

    def forward(h, carry):
        g, u = sums[lists[5, h]], sums[lists[6, h]]
        gate[h], up[h] = g, u
        hidden[h] = (g * jax.nn.sigmoid(g) * u).astype(jnp.bfloat16)
        return carry

    lax.fori_loop(0, HB, forward, 0)

    products(3, 0, PAIRS[3], hidden, False)(zero)
    gather_blocks(3, ob)
    red_o = reduce_rows(ob, 0, R_O)
    red_o.start()
    red_o.more()
    gg.cp.wait_recv()
    gg.cm.wait_recv()
    gg.e.wait_recv()

    red_g = [reduce_grads(k) for k in range(3)]
    red_y = [PairFirst(k) for k in range(3)]

    def head(k):
        slot_grads(k, 1 - core, (0, 1))
        core_send(k, (0, 1))
        slot_grads(k, core, (0, 1))
        slot_grads(k, 1 - core, (2, 3))
        core_send(k, (2, 3))
        core_add(k, 0)
        red_g[k].start()
        core_add(k, 1)
        send(red_y[k].y)

    def tail(k):
        slot_grads(k, core, (2, 3))
        slot_grads(k, 1 - core, (4, 5))
        core_send(k, (4, 5))
        core_add(k, 2)
        core_add(k, 3)
        red_g[k].more()
        slot_grads(k, core, (4, 5))
        core_add(k, 4)
        core_add(k, 5)

    head(2)
    tail(2)
    products(2, 0, PAIRS[2], gb, True)(zero)

    def backward(h, carry):
        g, u, hg = gate[h], up[h], sums[lists[7, h]]
        sig = jax.nn.sigmoid(g)
        rows[h] = (hg * u * sig * (1.0 + g * (1.0 - sig))).astype(jnp.bfloat16)
        rows[h + HB] = (hg * (g * sig)).astype(jnp.bfloat16)
        return carry

    lax.fori_loop(0, HB, backward, 0)
    head(0)
    red_g[2].relay()
    tail(0)
    red_y[2].ring()
    red_o.relay()
    products(4, 0, PAIRS[4], rows, True)(zero)
    gather_blocks(4, ib)
    red_i = reduce_rows(ib, 1, R_I)
    red_i.start()
    red_i.more()
    red_g[2].cross()
    head(1)
    red_g[0].relay()
    red_y[2].relay()
    tail(1)
    red_y[0].ring()
    red_o.cross()

    def finish_rows(red, out):
        for i in range(8):
            out[:, i * B : (i + 1) * B] = red.total(i).astype(jnp.bfloat16)


    def finish_grads(k):
        red = red_g[k]
        count = counts[0, k]

        def update(source, shift, i, carry):
            g = source.total(i)
            i = i + shift
            alive = (d * 6 + i < count).astype(jnp.float32)
            m = 0.9 * mom[0, k, i] + 0.1 * g
            v = 0.95 * mom[1, k, i] + 0.05 * g * g
            out_u[k, i] = alive * m / (jnp.sqrt(v) + EPSILON)
            return carry

        lax.fori_loop(0, 2, functools.partial(update, red_y[k], 4), 0)
        red.m.wait_recv()
        lax.fori_loop(0, 4, functools.partial(update, red, 0), 0)

    def end_pair_first(k):
        red_y[k].bp.wait_recv()
        red_y[k].bm.wait_recv()

    local(first, mom.at[0], L_M).wait()
    local(second, mom.at[1], L_M + 1).wait()
    end_pair_first(2)
    finish_grads(2)
    red_y[0].relay()
    red_y[1].ring()
    red_i.relay()
    red_g[1].relay()
    red_g[0].cross()
    red_o.m.wait_recv()
    finish_rows(red_o, out_o)
    red_y[1].relay()
    end_pair_first(0)
    finish_grads(0)
    red_g[1].cross()
    red_i.cross()
    end_pair_first(1)
    finish_grads(1)
    red_i.m.wait_recv()
    finish_rows(red_i, out_i)
    for copy in sent:
        copy.wait_send()


def store(*refs):
    src, dst, sem = refs[:3], refs[3:6], refs[6]
    copies = [pltpu.make_async_copy(s, o, sem.at[i]) for i, (s, o) in enumerate(zip(src, dst))]
    for copy in copies:
        copy.start()
    for copy in copies:
        copy.wait()


def local_step(inputs, out_grad, weights, block_index, block_counts, first_moment, second_moment):
    index = jnp.transpose(block_index, (0, 2, 1))
    any_, smem, vmem = (
        pl.BlockSpec(memory_space=s) for s in (pl.ANY, pltpu.SMEM, pltpu.VMEM)
    )
    f32, bf16, i32 = jnp.float32, jnp.bfloat16, jnp.int32
    blocks = lambda *n, dtype=bf16: pltpu.VMEM((*n, B, B), dtype)
    dma = pltpu.SemaphoreType.DMA
    shapes = (
        jax.ShapeDtypeStruct(inputs.shape, bf16),
        jax.ShapeDtypeStruct(inputs.shape, bf16),
        jax.ShapeDtypeStruct(first_moment.shape, f32),
    )
    results = pl.pallas_call(
        kernel,
        out_shape=shapes,
        in_specs=[any_, any_, any_, any_, smem, any_, any_],
        out_specs=[vmem, vmem, vmem],
        scratch_shapes=[
            blocks(DB),
            blocks(DB),
            blocks(3 * CAP + 1),
            blocks(ZERO + 1, dtype=f32),
            blocks(HB, dtype=f32),
            blocks(HB, dtype=f32),
            blocks(HB),
            blocks(2 * HB),
            blocks(DB),
            blocks(DB),
            blocks(2, 3 * 48),
            blocks(3 * 48),
            blocks(2, 2, 8),
            blocks(2, 2, 2, 8),
            blocks(2, 8),
            blocks(3, 2, 4),
            blocks(3, 2, 2, 4),
            blocks(3, 4),
            blocks(3, 8),
            blocks(3, 2, 1),
            blocks(3, 2, 2),
            blocks(2, 3, 6, dtype=f32),
            pltpu.VMEM((3, 2, CAP), i32),
            pltpu.SMEM((3, 2, CAP), i32),
            pltpu.VMEM((16, 2 * B), i32),
            pltpu.SMEM((16, 2 * B), i32),
            dma((N_LOCAL,)),
            dma((N_REMOTE,)),
            dma((N_REMOTE,)),
        ],
        compiler_params=pltpu.CompilerParams(
            collective_id=0, has_side_effects=True, vmem_limit_bytes=63_000_000
        ),
    )(inputs, out_grad, weights, index, block_counts, first_moment, second_moment)
    return pl.pallas_call(
        store,
        out_shape=shapes,
        in_specs=[vmem, vmem, vmem],
        out_specs=[any_, any_, any_],
        scratch_shapes=[dma((3,))],
    )(*results)


def solution(mesh):
    in_specs = (
        P("dp", "tensor"),
        P("dp", "tensor"),
        P(None, "tensor", None, None),
        P(None, "tensor", None),
        P("tensor", None),
        P(None, ("tensor", "dp"), None, None),
        P(None, ("tensor", "dp"), None, None),
    )
    out_specs = (P("dp", "tensor"), P("dp", "tensor"), P(None, ("tensor", "dp"), None, None))
    return jax.shard_map(local_step, mesh=mesh, in_specs=in_specs, out_specs=out_specs, check_vma=False)
```

```python
import functools

import jax
import jax.numpy as jnp
from jax import lax
from jax.experimental import pallas as pl
from jax.experimental.pallas import tpu as pltpu
from jax.sharding import PartitionSpec as P

MESH = pl.DeviceIdType.MESH
EPSILON = 1e-08
HB = 14
CAP = 96
DB = 64
B = 128
PAIRS = (56, 56, 56, 80, 128)
UNROLL = (28, 28, 28, 20, 32)
BASE = (0, 64, 64, 0, 0)
ZERO = 128
NO_SLOT = 3 * CAP

L_X, L_OG, L_W, L_M, L_IDX, L_LIST = 0, 8, 16, 19, 21, 23
N_LOCAL = 25
R_X, R_OG, R_O, R_I, R_GA, R_GB, R_CORE = 0, 8, 16, 23, 30, 51, 66
N_REMOTE = 84


def kernel(
    inputs, out_grad, weights, index, counts, first, second,
    out_o, out_i, out_u,
    xb, gb, wb, sums, gate, up, hidden, rows, ob, ib, grads, core_in,
    ra_o, rb_o, rm_o, ra_g, rb_g, rm_g, ya_g, yr_g, yb_g, mom,
    index_v, pairs, lists_v, lists,
    lsem, ssem, rsem,
):
    d, t = lax.axis_index("dp"), lax.axis_index("tensor")
    core, px, yh = d % 2, (d // 2) % 4, d // 8
    z, yl = t // 2, t % 2
    dev_core = (d + 1 - 2 * core, t)
    dev_xp = (yh * 8 + ((px + 1) % 4) * 2 + core, t)
    dev_xm = (yh * 8 + ((px + 3) % 4) * 2 + core, t)
    dev_yh = ((1 - yh) * 8 + px * 2 + core, t)
    dev_zp = (d, ((z + 1) % 4) * 2 + yl)
    dev_zm = (d, ((z + 3) % 4) * 2 + yl)
    dev_yl = (d, t + 1 - 2 * yl)

    def local(src, dst, sem):
        return pltpu.make_async_copy(src, dst, lsem.at[sem])

    def remote(src, dst, sem, dev):
        return pltpu.make_async_remote_copy(
            src_ref=src, dst_ref=dst, send_sem=ssem.at[sem], recv_sem=rsem.at[sem],
            device_id=dev, device_id_type=MESH,
        )

    sent = []

    def send(copy):
        copy.start()
        sent.append(copy)

    for i in range(8):
        local(inputs.at[:, pl.ds(i * B, B)], xb.at[t * 8 + i], L_X + i).start()
    for i in range(8):
        local(out_grad.at[:, pl.ds(i * B, B)], gb.at[t * 8 + i], L_OG + i).start()
    barrier = pltpu.get_barrier_semaphore()
    for dev in (dev_core, dev_xp, dev_xm, dev_yh, dev_zp, dev_zm, dev_yl):
        pl.semaphore_signal(barrier, inc=1, device_id=dev, device_id_type=MESH)
    local(index, index_v, L_IDX).start()
    local(index, pairs, L_IDX + 1).start()
    wb[NO_SLOT] = jnp.zeros((B, B), jnp.bfloat16)
    sums[ZERO] = jnp.zeros((B, B), jnp.float32)
    pl.semaphore_wait(barrier, 7)

    class Gather:
        def __init__(self, buf, base):
            chunk = lambda zz, yy, lo=0, n=8: buf.at[pl.ds((((zz + 4) % 4) * 2 + yy) * 8 + lo, n)]
            mk = lambda ref, sem, dev: remote(ref, ref, base + sem, dev)
            other = 1 - yl
            self.a = mk(chunk(z, yl), 0, dev_yl)
            self.bp = mk(chunk(z, yl), 1, dev_zp)
            self.bm = mk(chunk(z, yl), 2, dev_zm)
            self.cp = mk(chunk(z, other), 3, dev_zp)
            self.cm = mk(chunk(z, other), 4, dev_zm)
            self.dp = mk(chunk(z - 1, yl, 0, 4), 5, dev_zp)
            self.dm = mk(chunk(z + 1, yl, 4, 4), 6, dev_zm)
            self.e = mk(chunk(z + 2, yl), 7, dev_yl)

    class Reduce:
        def __init__(self, part, pos, pair, dev_p, dev_m, dev_pair, ra, rb, rm, base):
            nxt, opp, prv = (pos + 1) % 4, (pos + 2) % 4, (pos + 3) % 4
            self.part, self.pos, self.pair = part, pos, pair
            self.nxt, self.prv = nxt, prv
            self.ra, self.rb, self.rm = ra, rb, rm
            self.ap = remote(part(0, opp), ra.at[0], base, dev_p)
            self.am = remote(part(1, opp), ra.at[1], base + 1, dev_m)
            self.bp0 = remote(part(0, nxt), rb.at[0, 0], base + 2, dev_p)
            self.bp1 = remote(part(1, nxt), rb.at[0, 1], base + 3, dev_p)
            self.bm0 = remote(part(0, prv), rb.at[1, 0], base + 4, dev_m)
            self.bm1 = remote(part(1, prv), rb.at[1, 1], base + 5, dev_m)
            self.m = remote(part(1 - pair, pos), rm, base + 6, dev_pair)
            self.n = rm.shape[0]

        def start(self):
            send(self.ap)
            send(self.am)

        def more(self):
            send(self.bp1)
            send(self.bm0)

        def relay(self):
            self.ap.wait_recv()
            add_into(self.part(0, self.nxt), self.ra.at[0], self.n)
            send(self.bp0)
            self.am.wait_recv()
            add_into(self.part(1, self.prv), self.ra.at[1], self.n)
            send(self.bm1)

        def cross(self):
            for b in (self.bp0, self.bp1, self.bm0, self.bm1):
                b.wait_recv()
            far = 1 - self.pair
            mine = self.part(far, self.pos)

            for i in range(self.n):
                v = mine[i].astype(jnp.float32) + self.rb[0, far, i].astype(jnp.float32)
                mine[i] = (v + self.rb[1, far, i].astype(jnp.float32)).astype(jnp.bfloat16)
            send(self.m)

        def total(self, i):
            mine = self.part(self.pair, self.pos)
            v = mine[i].astype(jnp.float32) + self.rb[0, self.pair, i].astype(jnp.float32)
            v = v + self.rb[1, self.pair, i].astype(jnp.float32)
            return v + self.rm[i].astype(jnp.float32)

    def add_into(dst, src, n):
        for i in range(n):
            dst[i] = (dst[i].astype(jnp.float32) + src[i].astype(jnp.float32)).astype(jnp.bfloat16)

    def products(which, lo, hi, left, back):
        dims = (((1,), (1,)), ((), ())) if back else (((1,), (0,)), ((), ()))
        unroll, base = UNROLL[which], BASE[which]

        def body(i, acc):
            for u in range(unroll):
                j = lo + i * unroll + u
                v, w = lists[which, 2 * j], lists[which, 2 * j + 1]
                prod = lax.dot_general(
                    jnp.concatenate([left[(v >> 9) & 127], left[(w >> 9) & 127]], axis=1),
                    jnp.concatenate([wb[v & 511], wb[w & 511]], axis=1 if back else 0),
                    dims,
                    preferred_element_type=jnp.float32,
                )
                acc = acc * (v >> 16).astype(jnp.float32) + prod
                sums[base + j] = acc
            return acc

        return lambda acc: lax.fori_loop(0, (hi - lo) // unroll, body, acc)

    zero = jnp.zeros((B, B), jnp.float32)

    def gather_blocks(which, dst):
        def body(i, carry):
            dst[i] = sums[lists[5 + which, i]].astype(jnp.bfloat16)
            return carry

        lax.fori_loop(0, DB, body, 0, unroll=16)

    def piece_of(n):
        nxt, opp, prv = (px + 1) % 4, (px + 2) % 4, (px + 3) % 4
        ring = (opp, None, nxt, prv, None, px)[n]
        pair = (None, 1 - yh, None, None, yh, None)[n]
        return ring, pair, ring * 8 if pair is None else 32 + pair * 8

    def slot_grads(k, parity, pieces):
        left, right, left_hidden, row_base = (
            (xb, rows, False, 0), (xb, rows, False, HB), (hidden, gb, True, 0)
        )[k]
        for n in pieces:
            ring, pair, block = piece_of(n)
            for i in range(8):
                if pair is None:
                    slot = ((i // 4) * 8 + ring * 2 + parity) * 6 + i % 4
                else:
                    slot = (pair * 8 + (i // 2) * 2 + parity) * 6 + 4 + i % 2
                f, h = pairs[k, 0, slot], pairs[k, 1, slot]
                li, ri = (h, f) if left_hidden else (f, h + row_base)
                g = lax.dot_general(
                    left[li], right[ri], (((0,), (0,)), ((), ())), preferred_element_type=jnp.float32
                )
                grads[parity, k * 48 + block + i] = g.astype(jnp.bfloat16)

    def core_piece(k, n):
        at = pl.ds(k * 48 + piece_of(n)[2], 8)
        return remote(grads.at[1 - core, at], core_in.at[at], R_CORE + k * 6 + n, dev_core), at

    def core_send(k, pieces):
        for n in pieces:
            send(core_piece(k, n)[0])

    def core_add(k, n):
        copy, at = core_piece(k, n)
        copy.wait_recv()
        add_into(grads.at[core, at], core_in.at[at], 8)

    def reduce_grads(k):
        part = lambda j, r: grads.at[core, pl.ds(k * 48 + (r * 2 + j) * 4, 4)]
        return Reduce(
            part, px, yh, dev_xp, dev_xm, dev_yh, ra_g.at[k], rb_g.at[k], rm_g.at[k], R_GA + 7 * k
        )

    class PairFirst:
        def __init__(self, k):
            nxt, opp, prv = (px + 1) % 4, (px + 2) % 4, (px + 3) % 4
            at = lambda y, x, j, n: grads.at[core, pl.ds(k * 48 + 32 + (y * 4 + x) * 2 + j, n)]
            base = R_GB + 5 * k
            self.mine, self.got = at(yh, 0, 0, 8), ya_g.at[k]
            self.y = remote(at(1 - yh, 0, 0, 8), ya_g.at[k], base, dev_yh)
            self.ap = remote(at(yh, opp, 0, 1), yr_g.at[k, 0], base + 1, dev_xp)
            self.am = remote(at(yh, opp, 1, 1), yr_g.at[k, 1], base + 2, dev_xm)
            self.bp = remote(at(yh, nxt, 0, 2), yb_g.at[k, 0], base + 3, dev_xp)
            self.bm = remote(at(yh, prv, 0, 2), yb_g.at[k, 1], base + 4, dev_xm)
            self.for_p, self.for_m, self.last = at(yh, nxt, 0, 1), at(yh, prv, 1, 1), at(yh, px, 0, 2)
            self.relayed, self.ends = yr_g.at[k], yb_g.at[k]

        def ring(self):
            self.y.wait_recv()
            add_into(self.mine, self.got, 8)
            send(self.ap)
            send(self.am)

        def relay(self):
            self.ap.wait_recv()
            add_into(self.for_p, self.relayed.at[0], 1)
            send(self.bp)
            self.am.wait_recv()
            add_into(self.for_m, self.relayed.at[1], 1)
            send(self.bm)

        def total(self, i):
            v = self.last[i].astype(jnp.float32) + self.ends[0, i].astype(jnp.float32)
            return v + self.ends[1, i].astype(jnp.float32)

    def reduce_rows(buf, which, base):
        part = lambda j, r: buf.at[pl.ds((r * 2 + j) * 8, 8)]
        return Reduce(
            part, z, yl, dev_zp, dev_zm, dev_yl, ra_o.at[which], rb_o.at[which], rm_o.at[which], base
        )

    def build_lists():
        n, wide = CAP, 2 * B
        row_i = lax.broadcasted_iota(jnp.int32, (n, n), 0)
        lane_i = lax.broadcasted_iota(jnp.int32, (n, n), 1)
        eye = row_i == lane_i
        earlier = lane_i < row_i
        later = lane_i > row_i
        lane1 = lax.broadcasted_iota(jnp.int32, (1, n), 1)
        place = lax.broadcasted_iota(jnp.int32, (n, wide), 1)
        group = lax.broadcasted_iota(jnp.int32, (n, wide), 1)

        def flag(m):
            return jnp.where(m, 1, 0)

        def spread(row):
            return jnp.broadcast_to(row, (n, n))

        def column(row):
            return jnp.sum(jnp.where(eye, spread(row), 0), axis=1, keepdims=True)

        def items(k, target, source, source_base):
            alive = lane1 < counts[0, k]
            key = jnp.where(alive, index_v[k, target : target + 1, :], DB)
            src = index_v[k, source : source + 1, :] + source_base
            return key, lane1 + k * CAP + (src << 9)

        def one_list(which, sets):
            keys = [key for key, _ in sets]
            cols = [column(key) for key in keys]
            m = len(sets)
            odd_last = []
            for b in range(m):
                same = [flag(cols[a] == spread(keys[b])) for a in range(m)]
                count = sum(jnp.sum(s, axis=0, keepdims=True) for s in same)
                rank = jnp.sum(jnp.where(later, same[b], 0), axis=0, keepdims=True)
                for a in range(b):
                    rank = rank + jnp.sum(same[a], axis=0, keepdims=True)
                odd_last.append(jnp.where(rank + 1 == count, count & 1, 0))
            filled = jnp.zeros((1, wide), jnp.int32)
            taken = jnp.zeros((1, wide), jnp.int32)
            last = jnp.full((1, wide), -1, jnp.int32)
            for a in range(m):
                before = jnp.zeros((n, 1), jnp.int32)
                rank = jnp.zeros((n, 1), jnp.int32)
                for b in range(m):
                    less = spread(keys[b]) < cols[a]
                    weight = spread(1 + odd_last[b])
                    before = before + jnp.sum(jnp.where(less, weight, 0), axis=1, keepdims=True)
                    same = flag(spread(keys[b]) == cols[a])
                    if b == a:
                        same = jnp.where(earlier, same, 0)
                    if b <= a:
                        rank = rank + jnp.sum(same, axis=1, keepdims=True)
                at = before + rank
                packed = column(sets[a][1]) + jnp.where(rank >= 2, 65536, 0)
                hit = at == place
                filled = filled + jnp.sum(jnp.where(hit, packed, 0), axis=0, keepdims=True)
                taken = taken + jnp.sum(flag(hit), axis=0, keepdims=True)
                step = at >> 1
                mine = jnp.where(cols[a] == group, step, -1)
                last = jnp.maximum(last, jnp.max(mine, axis=0, keepdims=True))
            entry = jnp.where(taken > 0, filled, NO_SLOT)
            lists_v[which : which + 1, :] = entry
            last = jnp.where(last < 0, ZERO, last + BASE[which])
            lists_v[5 + which : 6 + which, :] = last

        local(index, index_v, L_IDX).wait()
        one_list(0, [items(0, 1, 0, 0)])
        one_list(1, [items(1, 1, 0, 0)])
        one_list(2, [items(2, 1, 0, 0)])
        one_list(3, [items(2, 0, 1, 0)])
        one_list(4, [items(0, 0, 1, 0), items(1, 0, 1, HB)])
        copy = local(lists_v, lists, L_LIST)
        copy.start()
        copy.wait()
        local(index, pairs, L_IDX + 1).wait()

    gx, gg = Gather(xb, R_X), Gather(gb, R_OG)
    for i in range(8):
        local(inputs.at[:, pl.ds(i * B, B)], xb.at[t * 8 + i], L_X + i).wait()
    send(gx.bp)
    send(gx.bm)
    send(gx.a)
    for i in range(8):
        local(out_grad.at[:, pl.ds(i * B, B)], gb.at[t * 8 + i], L_OG + i).wait()
    send(gg.bp)
    send(gg.bm)
    send(gg.a)
    for k in range(3):
        local(weights.at[k], wb.at[pl.ds(k * CAP, CAP)], L_W + k).start()
    local(first, mom.at[0], L_M).start()
    local(second, mom.at[1], L_M + 1).start()
    build_lists()
    gx.bp.wait_recv()
    send(gx.dp)
    gx.bm.wait_recv()
    send(gx.dm)
    gg.bp.wait_recv()
    send(gg.dp)
    gg.bm.wait_recv()
    send(gg.dm)
    gx.a.wait_recv()
    send(gx.cp)
    send(gx.cm)
    gg.a.wait_recv()
    send(gg.cp)
    send(gg.cm)
    gx.dp.wait_recv()
    gx.dm.wait_recv()
    send(gx.e)
    gg.dp.wait_recv()
    gg.dm.wait_recv()
    send(gg.e)
    for k in range(3):
        local(weights.at[k], wb.at[pl.ds(k * CAP, CAP)], L_W + k).wait()
    gx.cp.wait_recv()
    gx.cm.wait_recv()
    gx.e.wait_recv()

    products(0, 0, PAIRS[0], xb, False)(zero)
    products(1, 0, PAIRS[1], xb, False)(zero)

    def forward(h, carry):
        g, u = sums[lists[5, h]], sums[lists[6, h]]
        gate[h], up[h] = g, u
        hidden[h] = (g * jax.nn.sigmoid(g) * u).astype(jnp.bfloat16)
        return carry

    lax.fori_loop(0, HB, forward, 0)

    products(3, 0, PAIRS[3], hidden, False)(zero)
    gather_blocks(3, ob)
    red_o = reduce_rows(ob, 0, R_O)
    red_o.start()
    red_o.more()
    gg.cp.wait_recv()
    gg.cm.wait_recv()
    gg.e.wait_recv()

    red_g = [reduce_grads(k) for k in range(3)]
    red_y = [PairFirst(k) for k in range(3)]

    def head(k):
        slot_grads(k, 1 - core, (0, 1))
        core_send(k, (0, 1))
        slot_grads(k, core, (0, 1))
        slot_grads(k, 1 - core, (2, 3))
        core_send(k, (2, 3))
        core_add(k, 0)
        red_g[k].start()
        core_add(k, 1)
        send(red_y[k].y)

    def tail(k):
        slot_grads(k, core, (2, 3))
        slot_grads(k, 1 - core, (4, 5))
        core_send(k, (4, 5))
        core_add(k, 2)
        core_add(k, 3)
        red_g[k].more()
        slot_grads(k, core, (4, 5))
        core_add(k, 4)
        core_add(k, 5)

    head(2)
    tail(2)
    products(2, 0, PAIRS[2], gb, True)(zero)

    def backward(h, carry):
        g, u, hg = gate[h], up[h], sums[lists[7, h]]
        sig = jax.nn.sigmoid(g)
        rows[h] = (hg * u * sig * (1.0 + g * (1.0 - sig))).astype(jnp.bfloat16)
        rows[h + HB] = (hg * (g * sig)).astype(jnp.bfloat16)
        return carry

    lax.fori_loop(0, HB, backward, 0)
    head(0)
    red_g[2].relay()
    tail(0)
    red_y[2].ring()
    red_o.relay()
    products(4, 0, PAIRS[4], rows, True)(zero)
    gather_blocks(4, ib)
    red_i = reduce_rows(ib, 1, R_I)
    red_i.start()
    red_i.more()
    red_g[2].cross()
    head(1)
    red_g[0].relay()
    red_y[2].relay()
    tail(1)
    red_y[0].ring()
    red_o.cross()
    red_g[1].relay()
    red_y[1].ring()
    red_i.relay()
    red_g[0].cross()

    def finish_rows(red, out):
        for i in range(8):
            out[:, i * B : (i + 1) * B] = red.total(i).astype(jnp.bfloat16)


    def finish_grads(k):
        red = red_g[k]
        count = counts[0, k]

        def update(source, shift, i, carry):
            g = source.total(i)
            i = i + shift
            alive = (d * 6 + i < count).astype(jnp.float32)
            m = 0.9 * mom[0, k, i] + 0.1 * g
            v = 0.95 * mom[1, k, i] + 0.05 * g * g
            out_u[k, i] = alive * m / (jnp.sqrt(v) + EPSILON)
            return carry

        lax.fori_loop(0, 2, functools.partial(update, red_y[k], 4), 0)
        red.m.wait_recv()
        lax.fori_loop(0, 4, functools.partial(update, red, 0), 0)

    def end_pair_first(k):
        red_y[k].bp.wait_recv()
        red_y[k].bm.wait_recv()

    local(first, mom.at[0], L_M).wait()
    local(second, mom.at[1], L_M + 1).wait()
    red_y[0].relay()
    red_o.m.wait_recv()
    finish_rows(red_o, out_o)
    end_pair_first(2)
    finish_grads(2)
    red_y[1].relay()
    red_g[1].cross()
    red_i.cross()
    end_pair_first(0)
    finish_grads(0)
    end_pair_first(1)
    finish_grads(1)
    red_i.m.wait_recv()
    finish_rows(red_i, out_i)
    for copy in sent:
        copy.wait_send()


def store(*refs):
    src, dst, sem = refs[:3], refs[3:6], refs[6]
    copies = [pltpu.make_async_copy(s, o, sem.at[i]) for i, (s, o) in enumerate(zip(src, dst))]
    for copy in copies:
        copy.start()
    for copy in copies:
        copy.wait()


def local_step(inputs, out_grad, weights, block_index, block_counts, first_moment, second_moment):
    index = jnp.transpose(block_index, (0, 2, 1))
    any_, smem, vmem = (
        pl.BlockSpec(memory_space=s) for s in (pl.ANY, pltpu.SMEM, pltpu.VMEM)
    )
    f32, bf16, i32 = jnp.float32, jnp.bfloat16, jnp.int32
    blocks = lambda *n, dtype=bf16: pltpu.VMEM((*n, B, B), dtype)
    dma = pltpu.SemaphoreType.DMA
    shapes = (
        jax.ShapeDtypeStruct(inputs.shape, bf16),
        jax.ShapeDtypeStruct(inputs.shape, bf16),
        jax.ShapeDtypeStruct(first_moment.shape, f32),
    )
    results = pl.pallas_call(
        kernel,
        out_shape=shapes,
        in_specs=[any_, any_, any_, any_, smem, any_, any_],
        out_specs=[vmem, vmem, vmem],
        scratch_shapes=[
            blocks(DB),
            blocks(DB),
            blocks(3 * CAP + 1),
            blocks(ZERO + 1, dtype=f32),
            blocks(HB, dtype=f32),
            blocks(HB, dtype=f32),
            blocks(HB),
            blocks(2 * HB),
            blocks(DB),
            blocks(DB),
            blocks(2, 3 * 48),
            blocks(3 * 48),
            blocks(2, 2, 8),
            blocks(2, 2, 2, 8),
            blocks(2, 8),
            blocks(3, 2, 4),
            blocks(3, 2, 2, 4),
            blocks(3, 4),
            blocks(3, 8),
            blocks(3, 2, 1),
            blocks(3, 2, 2),
            blocks(2, 3, 6, dtype=f32),
            pltpu.VMEM((3, 2, CAP), i32),
            pltpu.SMEM((3, 2, CAP), i32),
            pltpu.VMEM((16, 2 * B), i32),
            pltpu.SMEM((16, 2 * B), i32),
            dma((N_LOCAL,)),
            dma((N_REMOTE,)),
            dma((N_REMOTE,)),
        ],
        compiler_params=pltpu.CompilerParams(
            collective_id=0, has_side_effects=True, vmem_limit_bytes=63_000_000
        ),
    )(inputs, out_grad, weights, index, block_counts, first_moment, second_moment)
    return pl.pallas_call(
        store,
        out_shape=shapes,
        in_specs=[vmem, vmem, vmem],
        out_specs=[any_, any_, any_],
        scratch_shapes=[dma((3,))],
    )(*results)


def solution(mesh):
    in_specs = (
        P("dp", "tensor"),
        P("dp", "tensor"),
        P(None, "tensor", None, None),
        P(None, "tensor", None),
        P("tensor", None),
        P(None, ("tensor", "dp"), None, None),
        P(None, ("tensor", "dp"), None, None),
    )
    out_specs = (P("dp", "tensor"), P("dp", "tensor"), P(None, ("tensor", "dp"), None, None))
    return jax.shard_map(local_step, mesh=mesh, in_specs=in_specs, out_specs=out_specs, check_vma=False)
```
